32 devices in a mesh: line: 2 (over x), track: 16 (over z, y, core).
Axes of the slice: x: 2, y: 2, z: 4, core: 2. Of those that a mesh axis runs over, the one named last changes fastest.
Arguments:
- radiance: bfloat16 [2, 64, 224, 1000], P('line', 'track'), may hold values from -40 to 40, as said below
Outputs:
- cleaned: bfloat16 [2, 64, 224, 1000], P('line', 'track')
- filter_matrix: float32 [224, 224], replicated
The draws below stay inside these ranges and needn't reach their ends.
Inputs may be any that keep to these rules, and one draw needn't show every extreme that they name: `radiance`: every flightline, band and column carries a column offset, a column gain and pixel noise, so no column is constant along track.
All inputs are finite; a program needn't handle non-finite values.
Results may differ from the reference program's by a relative error of at most 0.0045.
Values may be sent and summed in bfloat16 or wider, within the bound.
A program may use at most 64 MiB of HBM per device.

```python
import math
import jax
import jax.numpy as jnp
from jax import lax

BANDS = 224
COLS = 1000
NCOMP = 40
ITERS = 4
ROWS = 64
LINES = 2


def draw_radiance(key, part):
    line_axis = jnp.arange(LINES, dtype=jnp.float32)[:, None, None, None]
    row_axis = jnp.arange(ROWS, dtype=jnp.float32)[None, :, None, None]
    band_axis = jnp.arange(BANDS, dtype=jnp.float32)[None, None, :, None]
    scene = jnp.zeros((LINES, ROWS, BANDS, COLS), jnp.float32)
    for term in range(8):
        sub_keys = jax.random.split(jax.random.fold_in(key, term + 1), 5)
        amplitude = jax.random.normal(sub_keys[0], (LINES, 1, 1, COLS), jnp.float32)
        column_phase = jax.random.uniform(sub_keys[1], (LINES, 1, 1, COLS), jnp.float32, 0.0, 6.2831853)
        along_rate = jax.random.uniform(sub_keys[2], (LINES, 1, 1, 1), jnp.float32, 0.02, 0.1)
        band_rate = jax.random.uniform(sub_keys[3], (LINES, 1, 1, 1), jnp.float32, 0.5, 1.5) * (term + 1)
        band_phase = jax.random.uniform(sub_keys[4], (LINES, 1, 1, 1), jnp.float32, 0.0, 6.2831853)
        scene = scene + amplitude * jnp.cos(along_rate * row_axis + column_phase) * jnp.cos(3.14159265 * band_rate * band_axis / BANDS + band_phase)
    base_keys = jax.random.split(jax.random.fold_in(key, 100), 4)
    noise_level = jnp.exp(jax.random.uniform(base_keys[0], (LINES, 1, BANDS, 1), jnp.float32, math.log(0.15), math.log(0.6)))
    jitter = jax.random.normal(base_keys[1], (LINES, ROWS, BANDS, COLS), jnp.float32)
    ramp = (1.0 + 2.0 * row_axis / (ROWS - 1)) * (1.0 + 2.0 * line_axis / (LINES - 1))
    offset = 2.0 * jax.random.normal(base_keys[2], (LINES, 1, BANDS, COLS), jnp.float32)
    gain_map = jnp.exp(jax.random.uniform(base_keys[3], (LINES, 1, BANDS, COLS), jnp.float32, -0.5, 0.5))
    values = offset + gain_map * 0.4 * ramp * (0.5 * scene + noise_level * jitter)
    return jnp.clip(values, -40.0, 40.0).astype(jnp.bfloat16)


def setup_inputs(seed: int = 0) -> dict:
    seeds = jax.random.split(jax.random.key(seed), 2)
    return {
        "radiance": draw_radiance(jax.random.fold_in(seeds[1], 71), 0),
    }


EPSILON = 1e-05
HIGHEST = lax.Precision.HIGHEST

def destripe(flight_line):
    values = flight_line.astype(jnp.float32)
    first_sum = lax.optimization_barrier(jnp.sum(values, axis=0))
    second_sum = lax.optimization_barrier(jnp.sum(values * values, axis=0))
    col_mean = first_sum / ROWS
    col_spread = jnp.sqrt(second_sum / ROWS - col_mean * col_mean + EPSILON)
    band_mean = lax.optimization_barrier(jnp.mean(col_mean, axis=1))
    factor = lax.optimization_barrier(jnp.mean(col_spread, axis=1))[:, None] / col_spread
    centred = lax.optimization_barrier(((values - col_mean) * factor).astype(jnp.bfloat16))
    return (centred, band_mean)

def line_grams(flight_line):
    centred, band_mean = destripe(flight_line)
    widened = centred.astype(jnp.float32)
    steps_along = lax.optimization_barrier((widened[1:] - widened[:-1]).astype(jnp.bfloat16)).astype(jnp.float32)
    signal_part = jnp.einsum('rbc,rdc->bd', widened, widened)
    noise_part = jnp.einsum('rbc,rdc->bd', steps_along, steps_along)
    return (signal_part, noise_part)

def mnf_filter(signal_gram, noise_gram):
    noise_factor = jnp.linalg.cholesky(noise_gram)
    half_solved = jax.scipy.linalg.solve_triangular(noise_factor, signal_gram, lower=True)
    whitened = jax.scipy.linalg.solve_triangular(noise_factor, half_solved.T, lower=True)
    whitened = 0.5 * (whitened + whitened.T)
    subspace = jnp.eye(whitened.shape[0], NCOMP, dtype=jnp.float32)
    for iteration in range(ITERS):
        mapped = jnp.dot(whitened, subspace, precision=HIGHEST)
        inner_gram = jnp.dot(mapped.T, mapped, precision=HIGHEST)
        inner_factor = jnp.linalg.cholesky(inner_gram)
        subspace = jax.scipy.linalg.solve_triangular(inner_factor, mapped.T, lower=True).T
    forward_map = jax.scipy.linalg.solve_triangular(noise_factor.T, subspace, lower=False)
    backward_map = jnp.dot(noise_factor, subspace, precision=HIGHEST)
    return jnp.dot(forward_map, backward_map.T, precision=HIGHEST)

def reference(radiance):
    signal_parts, noise_parts = lax.map(line_grams, radiance)
    signal_gram = lax.optimization_barrier(jnp.sum(signal_parts, axis=0)) / (LINES * ROWS * COLS)
    noise_gram = lax.optimization_barrier(jnp.sum(noise_parts, axis=0)) / (2 * LINES * (ROWS - 1) * COLS)
    filter_matrix = mnf_filter(signal_gram, noise_gram)
    narrow = lax.optimization_barrier(filter_matrix.astype(jnp.bfloat16)).astype(jnp.float32)

    def restore(flight_line):
        centred, band_mean = destripe(flight_line)
        mixed = jnp.einsum('ab,rac->rbc', narrow, centred.astype(jnp.float32))
        return (band_mean[:, None] + mixed).astype(jnp.bfloat16)
    cleaned = lax.map(restore, radiance)
    return (cleaned, filter_matrix)
```

```python
import functools
import math

import jax
import jax.numpy as jnp
from jax import lax
from jax.experimental import pallas as pl
from jax.experimental.pallas import tpu as pltpu
from jax.sharding import PartitionSpec as P

NCOMP = 40
ITERS = 4


EPSILON = 1e-05
HIGHEST = lax.Precision.HIGHEST


PANEL = 32
GROUP = 8


def contract(left, right, left_axis, right_axis):
    return lax.dot_general(
        left, right, (((left_axis,), (right_axis,)), ((), ())),
        precision=HIGHEST, preferred_element_type=jnp.float32,
    )


def eliminate(panel, offset):
    size = panel.shape[0]
    row_ids = lax.broadcasted_iota(jnp.int32, (size, 128), 0)
    repeats = panel.shape[1] // 128
    tiles = [panel[:, t * 128:(t + 1) * 128] for t in range(repeats)]
    home, shift = divmod(offset, 128)
    scales = jnp.zeros((size, 128), jnp.float32)
    for start in range(0, size, GROUP):
        lanes = range(start, min(start + GROUP, size))
        columns = {}
        for k in lanes:
            tile, lane = divmod(offset + k, 128)
            columns[k] = jnp.broadcast_to(tiles[tile][:, lane:lane + 1], (size, 128))
        for k in lanes:
            pivot_row = jnp.broadcast_to(columns[k][k:k + 1], (size, 128))
            scales = jnp.where(row_ids == k, pivot_row, scales)
            step = jnp.where(row_ids > k, columns[k] * (1.0 / pivot_row), 0.0)
            for later in lanes:
                if later > k:
                    columns[later] = columns[later] - step * columns[later][k:k + 1]
            tiles = [tile - step * tile[k:k + 1] for tile in tiles]
    scales = 1.0 / jnp.sqrt(scales)
    return jnp.concatenate([tile * scales for tile in tiles], axis=1)


def mnf_kernel(signal_scale, noise_scale, kept, packed_ref, filter_ref, work):
    size = filter_ref.shape[0]
    wide = packed_ref.shape[0]
    packed = packed_ref[...]
    row_ids = lax.broadcasted_iota(jnp.int32, (wide, wide), 0)
    column_ids = lax.broadcasted_iota(jnp.int32, (wide, wide), 1)
    below = jnp.where((row_ids > column_ids) & (row_ids < size), packed, 0.0)
    above = jnp.where(row_ids < column_ids, packed, 0.0)
    diagonal = row_ids == column_ids
    noise = below + below.T + jnp.where(diagonal, packed, 0.0)
    signal = above + above.T + jnp.where(diagonal, packed[size:size + 1], 0.0)
    work[:, :wide] = noise[:size] * noise_scale
    work[:, wide:2 * wide] = jnp.where(diagonal, 1.0, 0.0)[:size]
    work[:, 2 * wide:] = signal[:size] * signal_scale
    for start in range(0, size, PANEL):
        end = min(start + PANEL, size)
        rows = eliminate(work[start:end, :], start)
        work[start:end, :] = rows
        if end < size:
            step = contract(rows[:, end:size], rows, 0, 0)
            work[end:, :] = work[end:, :] - step
    upper = work[:, :wide]
    upper = jnp.where(
        lax.broadcasted_iota(jnp.int32, (size, wide), 1)
        >= lax.broadcasted_iota(jnp.int32, (size, wide), 0),
        upper, 0.0,
    )
    inverse = work[:, wide:2 * wide]
    half_solved = work[:, 2 * wide:]
    margin = jnp.zeros((wide - size, wide), jnp.float32)
    inner = contract(
        jnp.concatenate([half_solved, margin], axis=0),
        jnp.concatenate([inverse, margin], axis=0), 1, 1,
    )
    whitened = 0.5 * (inner + inner.T)
    mapped = whitened[:kept]
    for iteration in range(ITERS):
        if iteration:
            mapped = contract(mapped, whitened, 1, 0)
        gram = contract(mapped, mapped, 1, 1)
        gram = jnp.concatenate([gram, jnp.zeros((kept, 128 - kept), jnp.float32)], axis=1)
        mapped = eliminate(jnp.concatenate([gram, mapped], axis=1), 0)[:, 128:]
    subspace = mapped[:, :size]
    forward = contract(subspace, inverse, 1, 0)
    backward = contract(subspace, upper, 1, 0)
    filter_ref[...] = contract(forward, backward, 0, 0)[:size, :size]


def mnf_filter(packed, size, signal_count, noise_count, kept):
    wide = packed.shape[0]
    return pl.pallas_call(
        functools.partial(mnf_kernel, 1.0 / signal_count, 1.0 / noise_count, kept),
        out_shape=jax.ShapeDtypeStruct((size, size), jnp.float32),
        in_specs=[pl.BlockSpec(memory_space=pltpu.VMEM)],
        out_specs=pl.BlockSpec(memory_space=pltpu.VMEM),
        scratch_shapes=[pltpu.VMEM((size, 3 * wide), jnp.float32)],
        name="mnf_filter",
    )(packed)


MESH = pl.DeviceIdType.MESH
VMEM_SPEC = pl.BlockSpec(memory_space=pltpu.VMEM)


def signal(semaphore, device):
    pl.semaphore_signal(semaphore, inc=1, device_id=device, device_id_type=MESH)


def merge(first, second, count):
    gap = second[0] - first[0]
    return first[0] + 0.5 * gap, first[1] + second[1] + (0.5 * count) * gap * gap


LIMIT = 40.0
FINE = 16.0
MEAN_STEP = 240.0 / math.log2(1.0 + LIMIT * FINE)
SPREAD_LOW, SPREAD_HIGH = math.log2(EPSILON), math.log2(LIMIT * LIMIT + 50.0)
SPREAD_STEP = 240.0 / (SPREAD_HIGH - SPREAD_LOW)
SPREAD_BASE = -0.5 * SPREAD_STEP * (SPREAD_HIGH + SPREAD_LOW)


def write_pair(ref, pair, count, *index):
    mean, total = pair
    code = jnp.exp2(MEAN_STEP * jnp.log2(1.0 + FINE * jnp.abs(mean)) - 120.0)
    ref[(*index, 0)] = jnp.where(mean < 0.0, -code, code).astype(ref.dtype)
    level = jnp.log2(total * (1.0 / count))
    ref[(*index, 1)] = jnp.exp2(SPREAD_STEP * level + SPREAD_BASE).astype(ref.dtype)


def read_codes(ref, *index):
    code = ref[(*index, 0)].astype(jnp.float32)
    size = jnp.exp2((jnp.log2(jnp.abs(code)) + 120.0) * (1.0 / MEAN_STEP)) - 1.0
    mean = jnp.where(code < 0.0, -size, size) * (1.0 / FINE)
    level = jnp.log2(ref[(*index, 1)].astype(jnp.float32)) - SPREAD_BASE
    return mean, level * (1.0 / SPREAD_STEP)


def read_pair(ref, count, *index):
    mean, level = read_codes(ref, *index)
    return mean, jnp.exp2(level) * count


def stats_kernel(
    tracks, x_ref, mean_ref, spread_ref, ahead_ref,
    out0, in0, own, out1, in1, out2, in2, gathered, other, send, recv, row_sem,
):
    chips = tracks // 2
    depth = chips // 2
    rows, bands, columns = x_ref.shape
    half = bands // 2
    width = in0.shape[-1]
    line = lax.axis_index("line")
    track = lax.axis_index("track")
    core, chip = lax.rem(track, 2), lax.div(track, 2)
    side, place = lax.rem(chip, 2), lax.div(chip, 2)
    own_rows = pl.ds(pl.multiple_of(core * half, 16), half)
    other_rows = pl.ds(pl.multiple_of((1 - core) * half, 16), half)
    partner = (line, chip * 2 + 1 - core)
    across = (line, (place * 2 + 1 - side) * 2 + core)

    def along(step):
        spot = lax.rem(place + step, depth)
        return spot, (line, (spot * 2 + side) * 2 + core)

    def copy(source, target, phase, sent, landed, device):
        return pltpu.make_async_remote_copy(
            src_ref=source, dst_ref=target, send_sem=send.at[phase, sent],
            recv_sem=recv.at[phase, landed], device_id=device, device_id_type=MESH,
        )

    def row_copy(device):
        return pltpu.make_async_remote_copy(
            src_ref=x_ref.at[0], dst_ref=ahead_ref, send_sem=row_sem.at[0],
            recv_sem=row_sem.at[1], device_id=device, device_id_type=MESH,
        )

    barrier = pltpu.get_barrier_semaphore()
    signal(barrier, partner)
    signal(barrier, across)
    for step in range(1, depth):
        signal(barrier, along(step)[1])
    has_before, has_after = track > 0, track < tracks - 1

    @pl.when(has_before)
    def _():
        signal(barrier, (line, track - 1))

    @pl.when(has_after)
    def _():
        signal(barrier, (line, track + 1))

    def local(band_rows, q):
        low = q * width
        high = min(low + width, columns)
        values = [x_ref[r, band_rows, low:high].astype(jnp.float32) for r in range(rows)]
        mean = sum(values[1:], values[0]) * (1.0 / rows)
        gaps = [value - mean for value in values]
        pair = mean, sum([gap * gap for gap in gaps], rows * EPSILON)
        if high - low < width:
            blank = jnp.ones((half, width - high + low), jnp.float32)
            pair = tuple(jnp.concatenate([item, blank], axis=1) for item in pair)
        return pair

    for q in range(chips):
        write_pair(out0, local(other_rows, q), rows, q)
    pl.semaphore_wait(barrier, depth + 1 + has_before.astype(jnp.int32) + has_after.astype(jnp.int32))

    started = []

    def launch(item):
        item.start()
        started.append(item)

    far = [(lax.rem(place + step, depth)) for step in range(1, depth + 1)]
    order = [spot * 2 + 1 - side for spot in far] + [spot * 2 + side for spot in far]
    for q in order:
        launch(copy(out0.at[q], in0.at[q], 0, q, q, partner))
    for q in range(chips):
        for k, item in enumerate(local(own_rows, q)):
            own[q, k] = item
    for spot in far:
        q = spot * 2 + 1 - side
        copy(in0.at[q], in0.at[q], 0, q, q, partner).wait_recv()
        pair = merge((own[q, 0], own[q, 1]), read_pair(in0, rows, q), rows)
        write_pair(out1, pair, 2 * rows, spot)
        launch(copy(out1.at[spot], in1.at[spot], 1, spot, spot, across))

    @pl.when(has_before)
    def _():
        row_copy((line, track - 1)).start()

    for step, spot in enumerate(far, 1):
        q = spot * 2 + side
        copy(in0.at[q], in0.at[q], 0, q, q, partner).wait_recv()
        pair = merge((own[q, 0], own[q, 1]), read_pair(in0, rows, q), rows)
        copy(in1.at[spot], in1.at[spot], 1, spot, spot, across).wait_recv()
        pair = merge(pair, read_pair(in1, 2 * rows, spot), 2 * rows)
        if step < depth:
            write_pair(out2, pair, 4 * rows, spot)
            launch(copy(out2.at[spot], in2.at[place], 2, spot, place, along(step)[1]))
    groups = [pair]
    for step in range(1, depth):
        spot, peer = along(step)
        copy(in2.at[spot], in2.at[spot], 2, spot, spot, peer).wait_recv()
        groups.append(read_pair(in2, 4 * rows, spot))
    mean = sum([group[0] for group in groups[1:]], groups[0][0]) * (1.0 / depth)
    total = sum([group[1] for group in groups[1:]], groups[0][1])
    for group in groups:
        total = total + (4.0 * rows) * (group[0] - mean) * (group[0] - mean)
    write_pair(gathered, (mean, total), tracks * rows, chip)

    def relay(q):
        launch(copy(gathered.at[q], other.at[q], 5, q, q, partner))

    def settle(ref, q, band_rows):
        mean, level = read_codes(ref, q)
        mean_ref[q, band_rows, :] = mean
        spread_ref[q, band_rows, :] = jnp.exp2(0.5 * level)

    for step in range(1, depth):
        launch(copy(gathered.at[chip], gathered.at[chip], 3, step, chip, along(step)[1]))
    for step in range(depth):
        spot, peer = along(step)
        q = spot * 2 + side
        if step:
            copy(gathered.at[q], gathered.at[q], 3, q, q, peer).wait_recv()
        launch(copy(gathered.at[q], gathered.at[q], 4, q, q, across))
        relay(q)
        settle(gathered, q, own_rows)
    for step in range(depth):
        q = along(step)[0] * 2 + 1 - side
        copy(gathered.at[q], gathered.at[q], 4, q, q, across).wait_recv()
        relay(q)
        settle(gathered, q, own_rows)
    for last in (side, 1 - side):
        for step in range(depth):
            q = along(step)[0] * 2 + last
            copy(other.at[q], other.at[q], 5, q, q, partner).wait_recv()
            settle(other, q, other_rows)

    @pl.when(has_after)
    def _():
        row_copy((line, track + 1)).wait_recv()

    @pl.when(jnp.logical_not(has_after))
    def _():
        ahead_ref[...] = x_ref[0]

    for item in started:
        item.wait_send()

    @pl.when(has_before)
    def _():
        row_copy((line, track - 1)).wait_send()


def column_stats(local_block, tracks):
    chips = tracks // 2
    depth = chips // 2
    _, bands, columns = local_block.shape
    width = -(-columns // (128 * chips)) * 128
    half = bands // 2

    def buffer(count, dtype=jnp.bfloat16):
        return pltpu.VMEM((count, 2, half, width), dtype)

    return pl.pallas_call(
        functools.partial(stats_kernel, tracks),
        out_shape=[
            jax.ShapeDtypeStruct((chips, bands, width), jnp.float32),
            jax.ShapeDtypeStruct((chips, bands, width), jnp.float32),
            jax.ShapeDtypeStruct((bands, columns), jnp.bfloat16),
        ],
        in_specs=[VMEM_SPEC],
        out_specs=[VMEM_SPEC] * 3,
        scratch_shapes=[buffer(chips), buffer(chips), buffer(chips, jnp.float32)]
        + [buffer(depth)] * 4 + [buffer(chips)] * 2
        + [pltpu.SemaphoreType.DMA((6, chips))] * 2 + [pltpu.SemaphoreType.DMA((2,))],
        compiler_params=pltpu.CompilerParams(collective_id=1, has_side_effects=True),
        name="column_stats",
    )(local_block)


def centre_kernel(
    keep_ref, x_ref, mean_ref, spread_ref, ahead_ref,
    centred_ref, band_ref, packed_ref, work, change,
):
    rows, bands, columns = x_ref.shape
    chips, _, width = mean_ref.shape
    band_mean = jnp.zeros((bands, 1), jnp.float32)
    band_spread = jnp.zeros((bands, 1), jnp.float32)
    for q in range(chips):
        span = min(width, columns - q * width)
        band_mean += jnp.sum(mean_ref[q, :, :span], axis=1, keepdims=True)
        band_spread += jnp.sum(spread_ref[q, :, :span], axis=1, keepdims=True)
    band_ref[...] = band_mean * (1.0 / columns)
    band_spread = band_spread * (1.0 / columns)
    for q in range(chips):
        low = q * width
        high = min(low + width, columns)
        span = high - low
        mean = mean_ref[q, :, :span]
        factor = band_spread / spread_ref[q, :, :span]

        def rounded(values):
            return ((values.astype(jnp.float32) - mean) * factor).astype(jnp.bfloat16)

        now = rounded(x_ref[0, :, low:high])
        for r in range(rows):
            work[r, :, low:high] = now
            centred_ref[r, :, low:high] = now
            later = rounded(x_ref[r + 1, :, low:high] if r + 1 < rows else ahead_ref[:, low:high])
            step = later.astype(jnp.float32) - now.astype(jnp.float32)
            if r + 1 == rows:
                step = step * keep_ref[0]
            change[r, :, low:high] = step.astype(jnp.bfloat16)
            now = later
    full = chips * width
    if full > columns:
        blank = jnp.zeros((rows, bands, full - columns), jnp.bfloat16)
        work[:, :, columns:] = blank
        change[:, :, columns:] = blank

    def gram(ref):
        total = jnp.zeros((bands, bands), jnp.float32)
        for r in range(rows):
            total += lax.dot_general(
                ref[r], ref[r], (((1,), (1,)), ((), ())), preferred_element_type=jnp.float32
            )
        return total

    signal_part, noise_part = gram(work), gram(change)
    row_ids = lax.broadcasted_iota(jnp.int32, (bands, bands), 0)
    column_ids = lax.broadcasted_iota(jnp.int32, (bands, bands), 1)
    diagonal = jnp.sum(
        jnp.where(row_ids == column_ids, signal_part, 0.0), axis=0, keepdims=True
    )
    packed_ref[...] = jnp.zeros(packed_ref.shape, jnp.float32)
    packed_ref[:bands, :bands] = jnp.where(row_ids < column_ids, signal_part, noise_part)
    packed_ref[bands:bands + 1, :bands] = diagonal


def centre(keep, local_block, mean, spread, ahead, height, wide):
    rows, bands, columns = local_block.shape
    full = mean.shape[0] * mean.shape[2]
    return pl.pallas_call(
        centre_kernel,
        out_shape=[
            jax.ShapeDtypeStruct(local_block.shape, jnp.bfloat16),
            jax.ShapeDtypeStruct((bands, 1), jnp.float32),
            jax.ShapeDtypeStruct((height, wide), jnp.float32),
        ],
        in_specs=[pl.BlockSpec(memory_space=pltpu.SMEM)] + [VMEM_SPEC] * 4,
        out_specs=[VMEM_SPEC] * 3,
        scratch_shapes=[pltpu.VMEM((rows, bands, full), jnp.bfloat16)] * 2,
        name="centre",
    )(keep, local_block, mean, spread, ahead)


def gram_kernel(lines, tracks, x_ref, out_ref, in0, mine, in1, total, in2, gathered, in3, send, recv):
    depth = tracks // 4
    line = lax.axis_index("line")
    track = lax.axis_index("track")
    core, chip = lax.rem(track, 2), lax.div(track, 2)
    side, place = lax.rem(chip, 2), lax.div(chip, 2)
    plane = lines * 2
    me = line * 2 + side
    partner = (line, chip * 2 + 1 - core)

    def beside(step):
        spot = lax.rem(me + step, plane)
        return spot, (lax.div(spot, 2), (place * 2 + lax.rem(spot, 2)) * 2 + core)

    def along(step):
        spot = lax.rem(place + step, depth)
        return spot, (line, (spot * 2 + side) * 2 + core)

    def copy(source, target, phase, sent, landed, device):
        return pltpu.make_async_remote_copy(
            src_ref=source, dst_ref=target, send_sem=send.at[phase, sent],
            recv_sem=recv.at[phase, landed], device_id=device, device_id_type=MESH,
        )

    barrier = pltpu.get_barrier_semaphore()
    signal(barrier, partner)
    for step in range(1, plane):
        signal(barrier, beside(step)[1])
    for step in range(1, depth):
        signal(barrier, along(step)[1])
    pl.semaphore_wait(barrier, plane + depth - 1)

    started = []

    def launch(item):
        item.start()
        started.append(item)

    for step in range(1, plane + 1):
        spot = beside(step)[0]
        launch(copy(x_ref.at[1 - core, spot], in0.at[spot], 0, spot, spot, partner))
    for step in range(1, plane + 1):
        spot, peer = beside(step)
        copy(in0.at[spot], in0.at[spot], 0, spot, spot, partner).wait_recv()
        mine[spot] = x_ref[core, spot] + in0[spot]
        if step < plane:
            launch(copy(mine.at[spot], in1.at[me], 1, spot, me, peer))
    piece = mine[me]
    for step in range(1, plane):
        spot, peer = beside(step)
        copy(in1.at[spot], in1.at[spot], 1, spot, spot, peer).wait_recv()
        piece = piece + in1[spot]
    total[...] = piece
    in2[place] = piece
    for step in range(1, depth):
        spot, peer = along(step)
        launch(copy(total, in2.at[place], 2, spot, place, peer))
    for step in range(1, depth):
        spot, peer = along(step)
        copy(in2.at[spot], in2.at[spot], 2, spot, spot, peer).wait_recv()
    piece = in2[0]
    for spot in range(1, depth):
        piece = piece + in2[spot]
    gathered[me] = piece
    for step in range(1, plane):
        launch(copy(gathered.at[me], gathered.at[me], 3, step, me, beside(step)[1]))
    launch(copy(gathered.at[me], in3.at[me], 4, me, me, partner))
    out_ref[core, me] = piece
    for step in range(1, plane):
        spot, peer = beside(step)
        copy(gathered.at[spot], gathered.at[spot], 3, spot, spot, peer).wait_recv()
        launch(copy(gathered.at[spot], in3.at[spot], 4, spot, spot, partner))
        out_ref[core, spot] = gathered[spot]
    for step in range(plane):
        spot = beside(step)[0]
        copy(in3.at[spot], in3.at[spot], 4, spot, spot, partner).wait_recv()
        out_ref[1 - core, spot] = in3[spot]
    for item in started:
        item.wait_send()


def gram_total(packed, lines, tracks):
    plane, depth = lines * 2, tracks // 4
    height, wide = packed.shape
    piece = (height // (2 * plane), wide)
    whole = (2, plane) + piece
    stack = pltpu.VMEM((plane,) + piece, jnp.float32)
    total = pl.pallas_call(
        functools.partial(gram_kernel, lines, tracks),
        out_shape=jax.ShapeDtypeStruct(whole, jnp.float32),
        in_specs=[VMEM_SPEC],
        out_specs=VMEM_SPEC,
        scratch_shapes=[
            stack, stack, stack, pltpu.VMEM(piece, jnp.float32),
            pltpu.VMEM((depth,) + piece, jnp.float32), stack, stack,
        ] + [pltpu.SemaphoreType.DMA((5, max(plane, depth)))] * 2,
        compiler_params=pltpu.CompilerParams(collective_id=0, has_side_effects=True),
        name="gram_total",
    )(packed.reshape(whole))
    return total.reshape(height, wide)


def body(radiance):
    local_block = radiance[0]
    row_count, size, column_count = local_block.shape
    track_count = lax.axis_size("track")
    line_count = lax.axis_size("line")
    total_rows = row_count * track_count
    mean, spread, ahead = column_stats(local_block, track_count)
    keep = (lax.axis_index("track") < track_count - 1).astype(jnp.float32).reshape(1)
    wide = (size // 128 + 1) * 128
    pieces = 16 * 2 * line_count
    height = -(-max(size + 1, wide) // pieces) * pieces
    centred, band_mean, packed = centre(keep, local_block, mean, spread, ahead, height, wide)
    packed = gram_total(packed, line_count, track_count)[:wide]
    signal_count = line_count * total_rows * column_count
    noise_count = 2 * line_count * (total_rows - 1) * column_count
    filter_matrix = mnf_filter(packed, size, signal_count, noise_count, NCOMP)
    narrow = filter_matrix.astype(jnp.bfloat16)
    mixed = jnp.einsum("ab,rac->rbc", narrow, centred, preferred_element_type=jnp.float32)
    cleaned = (band_mean + mixed).astype(jnp.bfloat16)
    return (cleaned[None], filter_matrix)


def solution(mesh):
    in_specs = (P("line", "track", None, None),)
    out_specs = (P("line", "track", None, None), P())
    return jax.shard_map(body, mesh=mesh, in_specs=in_specs, out_specs=out_specs, check_vma=False)
```

```python
import functools
import math

import jax
import jax.numpy as jnp
from jax import lax
from jax.experimental import pallas as pl
from jax.experimental.pallas import tpu as pltpu
from jax.sharding import PartitionSpec as P

NCOMP = 40
ITERS = 4


EPSILON = 1e-05
HIGHEST = lax.Precision.HIGHEST


PANEL = 32
GROUP = 16


def contract(left, right, left_axis, right_axis):
    return lax.dot_general(
        left, right, (((left_axis,), (right_axis,)), ((), ())),
        precision=HIGHEST, preferred_element_type=jnp.float32,
    )


def contract_fast(left, right, left_axis, right_axis):
    dims = (((left_axis,), (right_axis,)), ((), ()))
    high_left, high_right = left.astype(jnp.bfloat16), right.astype(jnp.bfloat16)
    low_left = (left - high_left.astype(jnp.float32)).astype(jnp.bfloat16)
    low_right = (right - high_right.astype(jnp.float32)).astype(jnp.bfloat16)

    def dot(a, b):
        return lax.dot_general(a, b, dims, preferred_element_type=jnp.float32)

    return dot(high_left, high_right) + (dot(high_left, low_right) + dot(low_left, high_right))


def eliminate(panel, offset):
    size = panel.shape[0]
    row_ids = lax.broadcasted_iota(jnp.int32, (8, 128), 0)
    repeats, pieces = panel.shape[1] // 128, size // 8
    tiles = [
        [panel[p * 8:(p + 1) * 8, t * 128:(t + 1) * 128] for p in range(pieces)]
        for t in range(repeats)
    ]
    scales = [jnp.zeros((8, 128), jnp.float32)] * pieces
    for start in range(0, size, GROUP):
        lanes = range(start, min(start + GROUP, size))
        columns = {}
        for k in lanes:
            tile, lane = divmod(offset + k, 128)
            columns[k] = [
                jnp.broadcast_to(tiles[tile][p][:, lane:lane + 1], (8, 128))
                if p >= k // 8 or k // 8 > p >= start // 8 else None for p in range(pieces)
            ]
        for k in lanes:
            home, line = divmod(k, 8)
            pivot_row = jnp.broadcast_to(columns[k][home][line:line + 1], (8, 128))
            scales[home] = jnp.where(row_ids == line, pivot_row, scales[home])
            inverse = 1.0 / pivot_row
            steps = {p: columns[k][p] * inverse for p in range(home, pieces)}
            steps[home] = jnp.where(row_ids > line, steps[home], 0.0)

            def reduce(item):
                row = jnp.broadcast_to(item[home][line:line + 1], (8, 128))
                return [
                    item[p] - steps[p] * row if p >= home else item[p] for p in range(pieces)
                ]

            for later in lanes:
                if later > k:
                    columns[later] = reduce(columns[later])
            tiles = [reduce(tile) for tile in tiles]
    scales = [1.0 / jnp.sqrt(item) for item in scales]
    return jnp.concatenate([
        jnp.concatenate([tile[p] * scales[p] for tile in tiles], axis=1) for p in range(pieces)
    ], axis=0)


def mnf_kernel(
    signal_scale, noise_scale, kept, packed_ref, filter_ref, narrow_ref, work, signal_work
):
    size = filter_ref.shape[0]
    wide = packed_ref.shape[0]
    packed = packed_ref[...]
    row_ids = lax.broadcasted_iota(jnp.int32, (wide, wide), 0)
    column_ids = lax.broadcasted_iota(jnp.int32, (wide, wide), 1)
    below = jnp.where((row_ids > column_ids) & (row_ids < size), packed, 0.0)
    above = jnp.where(row_ids < column_ids, packed, 0.0)
    diagonal = row_ids == column_ids
    noise = below + below.T + jnp.where(diagonal, packed, 0.0)
    signal = above + above.T + jnp.where(diagonal, packed[size:size + 1], 0.0)
    work[:, :wide] = noise[:size] * noise_scale
    work[:, wide:] = jnp.where(diagonal, 1.0, 0.0)[:size]
    signal_work[...] = signal * signal_scale
    for start in range(0, size, PANEL):
        end = min(start + PANEL, size)
        low = start // 128 * 128
        high = wide + -(-end // 128) * 128
        rows = eliminate(work[start:end, low:high], start - low)
        work[start:end, low:high] = rows
        if end < size:
            step = contract_fast(rows[:, end - low:size - low], rows, 0, 0)
            work[end:, low:high] = work[end:, low:high] - step
    upper = work[:, :wide]
    upper = jnp.where(
        lax.broadcasted_iota(jnp.int32, (size, wide), 1)
        >= lax.broadcasted_iota(jnp.int32, (size, wide), 0),
        upper, 0.0,
    )
    inverse = work[:, wide:]
    margin = jnp.zeros((wide - size, wide), jnp.float32)
    inverse_full = jnp.concatenate([inverse, margin], axis=0)
    half_solved = contract_fast(inverse_full, signal_work[...], 1, 0)
    inner = contract_fast(half_solved, inverse_full, 1, 1)
    whitened = 0.5 * (inner + inner.T)
    mapped = whitened[:kept]
    for iteration in range(ITERS):
        if iteration:
            mapped = contract_fast(mapped, whitened, 1, 0)
        gram = (contract if iteration + 1 == ITERS else contract_fast)(mapped, mapped, 1, 1)
        gram = jnp.concatenate([gram, jnp.zeros((kept, 128 - kept), jnp.float32)], axis=1)
        mapped = eliminate(jnp.concatenate([gram, mapped], axis=1), 0)[:, 128:]
    subspace = mapped[:, :size]
    forward = contract_fast(subspace, inverse, 1, 0)
    backward = contract_fast(subspace, upper, 1, 0)
    filter_matrix = contract_fast(forward, backward, 0, 0)
    filter_ref[...] = filter_matrix[:size, :size]
    narrow_ref[...] = filter_matrix.T[:size, :size].astype(jnp.bfloat16)


def mnf_filter(packed, size, signal_count, noise_count, kept):
    wide = packed.shape[0]
    return pl.pallas_call(
        functools.partial(mnf_kernel, 1.0 / signal_count, 1.0 / noise_count, kept),
        out_shape=[
            jax.ShapeDtypeStruct((size, size), jnp.float32),
            jax.ShapeDtypeStruct((size, size), jnp.bfloat16),
        ],
        in_specs=[pl.BlockSpec(memory_space=pltpu.VMEM)],
        out_specs=[pl.BlockSpec(memory_space=pltpu.VMEM)] * 2,
        scratch_shapes=[
            pltpu.VMEM((size, 2 * wide), jnp.float32), pltpu.VMEM((wide, wide), jnp.float32),
        ],
        name="mnf_filter",
    )(packed)


MESH = pl.DeviceIdType.MESH
VMEM_SPEC = pl.BlockSpec(memory_space=pltpu.VMEM)


def signal(semaphore, device):
    pl.semaphore_signal(semaphore, inc=1, device_id=device, device_id_type=MESH)


def merge(first, second, count):
    gap = second[0] - first[0]
    return first[0] + 0.5 * gap, first[1] + second[1] + (0.5 * count) * gap * gap


LIMIT = 40.0
FINE = 16.0
MEAN_STEP = 240.0 / math.log2(1.0 + LIMIT * FINE)
SPREAD_LOW, SPREAD_HIGH = math.log2(EPSILON), math.log2(LIMIT * LIMIT + 50.0)
SPREAD_STEP = 240.0 / (SPREAD_HIGH - SPREAD_LOW)
SPREAD_BASE = -0.5 * SPREAD_STEP * (SPREAD_HIGH + SPREAD_LOW)


def write_pair(ref, pair, count, *index):
    mean, total = pair
    code = jnp.exp2(MEAN_STEP * jnp.log2(1.0 + FINE * jnp.abs(mean)) - 120.0)
    ref[(*index, 0)] = jnp.where(mean < 0.0, -code, code).astype(ref.dtype)
    level = jnp.log2(total * (1.0 / count))
    ref[(*index, 1)] = jnp.exp2(SPREAD_STEP * level + SPREAD_BASE).astype(ref.dtype)


def read_codes(ref, *index):
    code = ref[(*index, 0)].astype(jnp.float32)
    size = jnp.exp2((jnp.log2(jnp.abs(code)) + 120.0) * (1.0 / MEAN_STEP)) - 1.0
    mean = jnp.where(code < 0.0, -size, size) * (1.0 / FINE)
    level = jnp.log2(ref[(*index, 1)].astype(jnp.float32)) - SPREAD_BASE
    return mean, level * (1.0 / SPREAD_STEP)


def read_pair(ref, count, *index):
    mean, level = read_codes(ref, *index)
    return mean, jnp.exp2(level) * count


def stats_kernel(
    tracks, x_ref, mean_ref, spread_ref, ahead_ref,
    out0, in0, own, out1, in1, out2, in2, gathered, other, passing, send, recv, row_sem,
):
    chips = tracks // 2
    depth = chips // 2
    rows, bands, columns = x_ref.shape
    half = bands // 2
    width = in0.shape[-1]
    line = lax.axis_index("line")
    track = lax.axis_index("track")
    core, chip = lax.rem(track, 2), lax.div(track, 2)
    side, place = lax.rem(chip, 2), lax.div(chip, 2)
    own_rows = pl.ds(pl.multiple_of(core * half, 16), half)
    other_rows = pl.ds(pl.multiple_of((1 - core) * half, 16), half)
    partner = (line, chip * 2 + 1 - core)
    across = (line, (place * 2 + 1 - side) * 2 + core)

    def along(step):
        spot = lax.rem(place + step, depth)
        return spot, (line, (spot * 2 + side) * 2 + core)

    def copy(source, target, phase, sent, landed, device):
        return pltpu.make_async_remote_copy(
            src_ref=source, dst_ref=target, send_sem=send.at[phase, sent],
            recv_sem=recv.at[phase, landed], device_id=device, device_id_type=MESH,
        )

    def row_copy(source, target, sent, landed, device):
        return pltpu.make_async_remote_copy(
            src_ref=source, dst_ref=target, send_sem=row_sem.at[0, sent],
            recv_sem=row_sem.at[1, landed], device_id=device, device_id_type=MESH,
        )

    inner, outer = core == 1, core == 0
    low_side, high_side = side == 0, side == 1
    hands_down = outer & low_side & (place > 0)
    passes_on = inner & low_side & (place < depth - 1)
    has_after = track < tracks - 1
    below = (line, (place * 2 - 2) * 2 + 1)
    above = (line, (place * 2 + 2) * 2)
    beyond = (line, place * 4 + 1)
    to_partner = row_copy(x_ref.at[0], ahead_ref, 0, 0, partner)
    to_below = row_copy(x_ref.at[0], passing, 1, 1, below)
    to_across = row_copy(passing, ahead_ref, 1, 0, across)
    to_beyond = row_copy(x_ref.at[0], ahead_ref, 0, 0, beyond)

    barrier = pltpu.get_barrier_semaphore()
    signal(barrier, partner)
    signal(barrier, across)
    for step in range(1, depth):
        signal(barrier, along(step)[1])

    @pl.when(outer & high_side)
    def _():
        signal(barrier, beyond)

    @pl.when(inner & low_side)
    def _():
        signal(barrier, (line, place * 4 + 2))

    @pl.when(hands_down)
    def _():
        signal(barrier, below)

    @pl.when(passes_on)
    def _():
        signal(barrier, above)

    def local(band_rows, q):
        low = q * width
        high = min(low + width, columns)
        values = [x_ref[r, band_rows, low:high].astype(jnp.float32) for r in range(rows)]
        mean = sum(values[1:], values[0]) * (1.0 / rows)
        gaps = [value - mean for value in values]
        pair = mean, sum([gap * gap for gap in gaps], rows * EPSILON)
        if high - low < width:
            blank = jnp.ones((half, width - high + low), jnp.float32)
            pair = tuple(jnp.concatenate([item, blank], axis=1) for item in pair)
        return pair

    for q in range(chips):
        write_pair(out0, local(other_rows, q), rows, q)
    greeted = (outer & high_side) | (inner & low_side)
    relayed = hands_down | passes_on
    pl.semaphore_wait(
        barrier, depth + 1 + greeted.astype(jnp.int32) + relayed.astype(jnp.int32)
    )

    @pl.when(hands_down)
    def _():
        to_below.start()


    started = []

    def launch(item):
        item.start()
        started.append(item)

    far = [(lax.rem(place + step, depth)) for step in range(1, depth + 1)]
    order = [spot * 2 + 1 - side for spot in far] + [spot * 2 + side for spot in far]
    for q in order:
        launch(copy(out0.at[q], in0.at[q], 0, q, q, partner))
    for q in range(chips):
        for k, item in enumerate(local(own_rows, q)):
            own[q, k] = item
    for spot in far:
        q = spot * 2 + 1 - side
        copy(in0.at[q], in0.at[q], 0, q, q, partner).wait_recv()
        pair = merge((own[q, 0], own[q, 1]), read_pair(in0, rows, q), rows)
        write_pair(out1, pair, 2 * rows, spot)
        launch(copy(out1.at[spot], in1.at[spot], 1, spot, spot, across))

    @pl.when(inner)
    def _():
        to_partner.start()

    @pl.when(outer & high_side)
    def _():
        to_beyond.start()

    @pl.when(passes_on)
    def _():
        row_copy(x_ref.at[0], passing, 1, 1, above).wait_recv()
        to_across.start()

    for step, spot in enumerate(far, 1):
        q = spot * 2 + side
        copy(in0.at[q], in0.at[q], 0, q, q, partner).wait_recv()
        pair = merge((own[q, 0], own[q, 1]), read_pair(in0, rows, q), rows)
        copy(in1.at[spot], in1.at[spot], 1, spot, spot, across).wait_recv()
        pair = merge(pair, read_pair(in1, 2 * rows, spot), 2 * rows)
        if step < depth:
            write_pair(out2, pair, 4 * rows, spot)
            launch(copy(out2.at[spot], in2.at[place], 2, spot, place, along(step)[1]))
    groups = [pair]
    for step in range(1, depth):
        spot, peer = along(step)
        copy(in2.at[spot], in2.at[spot], 2, spot, spot, peer).wait_recv()
        groups.append(read_pair(in2, 4 * rows, spot))
    mean = sum([group[0] for group in groups[1:]], groups[0][0]) * (1.0 / depth)
    total = sum([group[1] for group in groups[1:]], groups[0][1])
    for group in groups:
        total = total + (4.0 * rows) * (group[0] - mean) * (group[0] - mean)
    write_pair(gathered, (mean, total), tracks * rows, chip)

    def relay(q):
        launch(copy(gathered.at[q], other.at[q], 5, q, q, partner))

    def settle(ref, q, band_rows):
        mean, level = read_codes(ref, q)
        mean_ref[q, band_rows, :] = mean
        spread_ref[q, band_rows, :] = jnp.exp2(0.5 * level)

    for step in range(1, depth):
        launch(copy(gathered.at[chip], gathered.at[chip], 3, step, chip, along(step)[1]))
    for step in range(depth):
        spot, peer = along(step)
        q = spot * 2 + side
        if step:
            copy(gathered.at[q], gathered.at[q], 3, q, q, peer).wait_recv()
        launch(copy(gathered.at[q], gathered.at[q], 4, q, q, across))
        relay(q)
        settle(gathered, q, own_rows)
    for step in range(depth):
        q = along(step)[0] * 2 + 1 - side
        copy(gathered.at[q], gathered.at[q], 4, q, q, across).wait_recv()
        relay(q)
        settle(gathered, q, own_rows)
    for last in (side, 1 - side):
        for step in range(depth):
            q = along(step)[0] * 2 + last
            copy(other.at[q], other.at[q], 5, q, q, partner).wait_recv()
            settle(other, q, other_rows)

    @pl.when(has_after)
    def _():
        to_partner.wait_recv()

    @pl.when(jnp.logical_not(has_after))
    def _():
        ahead_ref[...] = x_ref[0]

    for item in started:
        item.wait_send()

    @pl.when(inner)
    def _():
        to_partner.wait_send()

    @pl.when(outer & high_side)
    def _():
        to_beyond.wait_send()

    @pl.when(hands_down)
    def _():
        to_below.wait_send()

    @pl.when(passes_on)
    def _():
        to_across.wait_send()


def column_stats(local_block, tracks):
    chips = tracks // 2
    depth = chips // 2
    _, bands, columns = local_block.shape
    width = -(-columns // (128 * chips)) * 128
    half = bands // 2

    def buffer(count, dtype=jnp.bfloat16):
        return pltpu.VMEM((count, 2, half, width), dtype)

    return pl.pallas_call(
        functools.partial(stats_kernel, tracks),
        out_shape=[
            jax.ShapeDtypeStruct((chips, bands, width), jnp.float32),
            jax.ShapeDtypeStruct((chips, bands, width), jnp.float32),
            jax.ShapeDtypeStruct((bands, columns), jnp.bfloat16),
        ],
        in_specs=[VMEM_SPEC],
        out_specs=[VMEM_SPEC] * 3,
        scratch_shapes=[buffer(chips), buffer(chips), buffer(chips, jnp.float32)]
        + [buffer(depth)] * 4 + [buffer(chips)] * 2
        + [pltpu.VMEM((bands, columns), jnp.bfloat16)]
        + [pltpu.SemaphoreType.DMA((6, chips))] * 2 + [pltpu.SemaphoreType.DMA((2, 2))],
        compiler_params=pltpu.CompilerParams(collective_id=1, has_side_effects=True),
        name="column_stats",
    )(local_block)


def centre_kernel(
    keep_ref, x_ref, mean_ref, spread_ref, ahead_ref,
    centred_ref, band_ref, packed_ref, work, change,
):
    rows, bands, columns = x_ref.shape
    chips, _, width = mean_ref.shape
    band_mean = jnp.zeros((bands, 1), jnp.float32)
    band_spread = jnp.zeros((bands, 1), jnp.float32)
    for q in range(chips):
        span = min(width, columns - q * width)
        band_mean += jnp.sum(mean_ref[q, :, :span], axis=1, keepdims=True)
        band_spread += jnp.sum(spread_ref[q, :, :span], axis=1, keepdims=True)
    band_ref[...] = band_mean * (1.0 / columns)
    band_spread = band_spread * (1.0 / columns)
    for q in range(chips):
        low = q * width
        high = min(low + width, columns)
        span = high - low
        mean = mean_ref[q, :, :span]
        factor = band_spread / spread_ref[q, :, :span]

        def rounded(values):
            return ((values.astype(jnp.float32) - mean) * factor).astype(jnp.bfloat16)

        now = rounded(x_ref[0, :, low:high])
        for r in range(rows):
            work[r, :, low:high] = now
            centred_ref[r, :, low:high] = now
            later = rounded(x_ref[r + 1, :, low:high] if r + 1 < rows else ahead_ref[:, low:high])
            step = later.astype(jnp.float32) - now.astype(jnp.float32)
            if r + 1 == rows:
                step = step * keep_ref[0]
            change[r, :, low:high] = step.astype(jnp.bfloat16)
            now = later
    full = chips * width
    if full > columns:
        blank = jnp.zeros((rows, bands, full - columns), jnp.bfloat16)
        work[:, :, columns:] = blank
        change[:, :, columns:] = blank

    def gram(ref):
        total = jnp.zeros((bands, bands), jnp.float32)
        for r in range(rows):
            total += lax.dot_general(
                ref[r], ref[r], (((1,), (1,)), ((), ())), preferred_element_type=jnp.float32
            )
        return total

    signal_part, noise_part = gram(work), gram(change)
    row_ids = lax.broadcasted_iota(jnp.int32, (bands, bands), 0)
    column_ids = lax.broadcasted_iota(jnp.int32, (bands, bands), 1)
    diagonal = jnp.sum(
        jnp.where(row_ids == column_ids, signal_part, 0.0), axis=0, keepdims=True
    )
    packed_ref[...] = jnp.zeros(packed_ref.shape, jnp.float32)
    packed_ref[:bands, :bands] = jnp.where(row_ids < column_ids, signal_part, noise_part)
    packed_ref[bands:bands + 1, :bands] = diagonal


def centre(keep, local_block, mean, spread, ahead, height, wide):
    rows, bands, columns = local_block.shape
    full = mean.shape[0] * mean.shape[2]
    return pl.pallas_call(
        centre_kernel,
        out_shape=[
            jax.ShapeDtypeStruct(local_block.shape, jnp.bfloat16),
            jax.ShapeDtypeStruct((bands, 1), jnp.float32),
            jax.ShapeDtypeStruct((height, wide), jnp.float32),
        ],
        in_specs=[pl.BlockSpec(memory_space=pltpu.SMEM)] + [VMEM_SPEC] * 4,
        out_specs=[VMEM_SPEC] * 3,
        scratch_shapes=[pltpu.VMEM((rows, bands, full), jnp.bfloat16)] * 2,
        name="centre",
    )(keep, local_block, mean, spread, ahead)


def gram_kernel(lines, tracks, x_ref, out_ref, in0, mine, in1, total, in2, gathered, in3, send, recv):
    depth = tracks // 4
    line = lax.axis_index("line")
    track = lax.axis_index("track")
    core, chip = lax.rem(track, 2), lax.div(track, 2)
    side, place = lax.rem(chip, 2), lax.div(chip, 2)
    plane = lines * 2
    me = line * 2 + side
    partner = (line, chip * 2 + 1 - core)

    def beside(step):
        spot = lax.rem(me + step, plane)
        return spot, (lax.div(spot, 2), (place * 2 + lax.rem(spot, 2)) * 2 + core)

    def along(step):
        spot = lax.rem(place + step, depth)
        return spot, (line, (spot * 2 + side) * 2 + core)

    def copy(source, target, phase, sent, landed, device):
        return pltpu.make_async_remote_copy(
            src_ref=source, dst_ref=target, send_sem=send.at[phase, sent],
            recv_sem=recv.at[phase, landed], device_id=device, device_id_type=MESH,
        )

    barrier = pltpu.get_barrier_semaphore()
    signal(barrier, partner)
    for step in range(1, plane):
        signal(barrier, beside(step)[1])
    for step in range(1, depth):
        signal(barrier, along(step)[1])
    pl.semaphore_wait(barrier, plane + depth - 1)

    started = []

    def launch(item):
        item.start()
        started.append(item)

    for step in range(1, plane + 1):
        spot = beside(step)[0]
        launch(copy(x_ref.at[1 - core, spot], in0.at[spot], 0, spot, spot, partner))
    for step in range(1, plane + 1):
        spot, peer = beside(step)
        copy(in0.at[spot], in0.at[spot], 0, spot, spot, partner).wait_recv()
        mine[spot] = x_ref[core, spot] + in0[spot]
        if step < plane:
            launch(copy(mine.at[spot], in1.at[me], 1, spot, me, peer))
    piece = mine[me]
    for step in range(1, plane):
        spot, peer = beside(step)
        copy(in1.at[spot], in1.at[spot], 1, spot, spot, peer).wait_recv()
        piece = piece + in1[spot]
    total[...] = piece
    in2[place] = piece
    for step in range(1, depth):
        spot, peer = along(step)
        launch(copy(total, in2.at[place], 2, spot, place, peer))
    for step in range(1, depth):
        spot, peer = along(step)
        copy(in2.at[spot], in2.at[spot], 2, spot, spot, peer).wait_recv()
    piece = in2[0]
    for spot in range(1, depth):
        piece = piece + in2[spot]
    gathered[me] = piece
    for step in range(1, plane):
        launch(copy(gathered.at[me], gathered.at[me], 3, step, me, beside(step)[1]))
    launch(copy(gathered.at[me], in3.at[me], 4, me, me, partner))
    out_ref[core, me] = piece
    for step in range(1, plane):
        spot, peer = beside(step)
        copy(gathered.at[spot], gathered.at[spot], 3, spot, spot, peer).wait_recv()
        launch(copy(gathered.at[spot], in3.at[spot], 4, spot, spot, partner))
        out_ref[core, spot] = gathered[spot]
    for step in range(plane):
        spot = beside(step)[0]
        copy(in3.at[spot], in3.at[spot], 4, spot, spot, partner).wait_recv()
        out_ref[1 - core, spot] = in3[spot]
    for item in started:
        item.wait_send()


def gram_total(packed, lines, tracks):
    plane, depth = lines * 2, tracks // 4
    height, wide = packed.shape
    piece = (height // (2 * plane), wide)
    whole = (2, plane) + piece
    stack = pltpu.VMEM((plane,) + piece, jnp.float32)
    total = pl.pallas_call(
        functools.partial(gram_kernel, lines, tracks),
        out_shape=jax.ShapeDtypeStruct(whole, jnp.float32),
        in_specs=[VMEM_SPEC],
        out_specs=VMEM_SPEC,
        scratch_shapes=[
            stack, stack, stack, pltpu.VMEM(piece, jnp.float32),
            pltpu.VMEM((depth,) + piece, jnp.float32), stack, stack,
        ] + [pltpu.SemaphoreType.DMA((5, max(plane, depth)))] * 2,
        compiler_params=pltpu.CompilerParams(collective_id=0, has_side_effects=True),
        name="gram_total",
    )(packed.reshape(whole))
    return total.reshape(height, wide)


def restore_kernel(narrow_ref, band_ref, centred_ref, cleaned_ref):
    mixed = jnp.dot(narrow_ref[...], centred_ref[0], preferred_element_type=jnp.float32)
    cleaned_ref[0] = (band_ref[...] + mixed).astype(jnp.bfloat16)


def restore(narrow, band_mean, centred):
    rows, bands, columns = centred.shape
    block = pl.BlockSpec((1, bands, columns), lambda r: (r, 0, 0))
    return pl.pallas_call(
        restore_kernel,
        grid=(rows,),
        out_shape=jax.ShapeDtypeStruct(centred.shape, jnp.bfloat16),
        in_specs=[
            pl.BlockSpec((bands, bands), lambda r: (0, 0)),
            pl.BlockSpec((bands, 1), lambda r: (0, 0)),
            block,
        ],
        out_specs=block,
        name="restore",
    )(narrow, band_mean, centred)


def body(radiance):
    local_block = radiance[0]
    row_count, size, column_count = local_block.shape
    track_count = lax.axis_size("track")
    line_count = lax.axis_size("line")
    total_rows = row_count * track_count
    mean, spread, ahead = column_stats(local_block, track_count)
    keep = (lax.axis_index("track") < track_count - 1).astype(jnp.float32).reshape(1)
    wide = (size // 128 + 1) * 128
    pieces = 16 * 2 * line_count
    height = -(-max(size + 1, wide) // pieces) * pieces
    centred, band_mean, packed = centre(keep, local_block, mean, spread, ahead, height, wide)
    packed = gram_total(packed, line_count, track_count)[:wide]
    signal_count = line_count * total_rows * column_count
    noise_count = 2 * line_count * (total_rows - 1) * column_count
    filter_matrix, narrow = mnf_filter(packed, size, signal_count, noise_count, NCOMP)
    cleaned = restore(narrow, band_mean, centred)
    return (cleaned[None], filter_matrix)


def solution(mesh):
    in_specs = (P("line", "track", None, None),)
    out_specs = (P("line", "track", None, None), P())
    return jax.shard_map(body, mesh=mesh, in_specs=in_specs, out_specs=out_specs, check_vma=False)
```

```python
import functools
import math

import jax
import jax.numpy as jnp
from jax import lax
from jax.experimental import pallas as pl
from jax.experimental.pallas import tpu as pltpu
from jax.sharding import PartitionSpec as P

NCOMP = 40
ITERS = 4


EPSILON = 1e-05
HIGHEST = lax.Precision.HIGHEST


PANEL = 32
GROUP = 16


def contract(left, right, left_axis, right_axis):
    return lax.dot_general(
        left, right, (((left_axis,), (right_axis,)), ((), ())),
        precision=HIGHEST, preferred_element_type=jnp.float32,
    )


def contract_fast(left, right, left_axis, right_axis):
    dims = (((left_axis,), (right_axis,)), ((), ()))
    high_left, high_right = left.astype(jnp.bfloat16), right.astype(jnp.bfloat16)
    low_left = (left - high_left.astype(jnp.float32)).astype(jnp.bfloat16)
    low_right = (right - high_right.astype(jnp.float32)).astype(jnp.bfloat16)

    def dot(a, b):
        return lax.dot_general(a, b, dims, preferred_element_type=jnp.float32)

    return dot(high_left, high_right) + (dot(high_left, low_right) + dot(low_left, high_right))


def eliminate(panel, offset):
    size = panel.shape[0]
    row_ids = lax.broadcasted_iota(jnp.int32, (8, 128), 0)
    repeats, pieces = panel.shape[1] // 128, size // 8
    tiles = [
        [panel[p * 8:(p + 1) * 8, t * 128:(t + 1) * 128] for p in range(pieces)]
        for t in range(repeats)
    ]
    scales = [jnp.zeros((8, 128), jnp.float32)] * pieces
    for start in range(0, size, GROUP):
        lanes = range(start, min(start + GROUP, size))
        columns = {}
        for k in lanes:
            tile, lane = divmod(offset + k, 128)
            columns[k] = [
                jnp.broadcast_to(tiles[tile][p][:, lane:lane + 1], (8, 128))
                if p >= k // 8 or k // 8 > p >= start // 8 else None for p in range(pieces)
            ]
        for k in lanes:
            home, line = divmod(k, 8)
            pivot_row = jnp.broadcast_to(columns[k][home][line:line + 1], (8, 128))
            scales[home] = jnp.where(row_ids == line, pivot_row, scales[home])
            inverse = 1.0 / pivot_row
            steps = {p: columns[k][p] * inverse for p in range(home, pieces)}
            steps[home] = jnp.where(row_ids > line, steps[home], 0.0)

            def reduce(item):
                row = jnp.broadcast_to(item[home][line:line + 1], (8, 128))
                return [
                    item[p] - steps[p] * row if p >= home else item[p] for p in range(pieces)
                ]

            for later in lanes:
                if later > k:
                    columns[later] = reduce(columns[later])
            tiles = [reduce(tile) for tile in tiles]
    scales = [1.0 / jnp.sqrt(item) for item in scales]
    return jnp.concatenate([
        jnp.concatenate([tile[p] * scales[p] for tile in tiles], axis=1) for p in range(pieces)
    ], axis=0)


def mnf_kernel(
    signal_scale, noise_scale, kept, packed_ref, filter_ref, narrow_ref, work, signal_work
):
    size = filter_ref.shape[0]
    wide = packed_ref.shape[0]
    packed = packed_ref[...]
    row_ids = lax.broadcasted_iota(jnp.int32, (wide, wide), 0)
    column_ids = lax.broadcasted_iota(jnp.int32, (wide, wide), 1)
    below = jnp.where((row_ids > column_ids) & (row_ids < size), packed, 0.0)
    above = jnp.where(row_ids < column_ids, packed, 0.0)
    diagonal = row_ids == column_ids
    noise = below + below.T + jnp.where(diagonal, packed, 0.0)
    signal = above + above.T + jnp.where(diagonal, packed[size:size + 1], 0.0)
    work[:, :wide] = noise[:size] * noise_scale
    work[:, wide:] = jnp.where(diagonal, 1.0, 0.0)[:size]
    signal_work[...] = signal * signal_scale
    for start in range(0, size, PANEL):
        end = min(start + PANEL, size)
        low = start // 128 * 128
        high = wide + -(-end // 128) * 128
        rows = eliminate(work[start:end, low:high], start - low)
        work[start:end, low:high] = rows
        if end < size:
            step = contract_fast(rows[:, end - low:size - low], rows, 0, 0)
            work[end:, low:high] = work[end:, low:high] - step
    upper = work[:, :wide]
    upper = jnp.where(
        lax.broadcasted_iota(jnp.int32, (size, wide), 1)
        >= lax.broadcasted_iota(jnp.int32, (size, wide), 0),
        upper, 0.0,
    )
    inverse = work[:, wide:]
    margin = jnp.zeros((wide - size, wide), jnp.float32)
    inverse_full = jnp.concatenate([inverse, margin], axis=0)
    half_solved = contract_fast(inverse_full, signal_work[...], 1, 0)
    inner = contract_fast(half_solved, inverse_full, 1, 1)
    whitened = 0.5 * (inner + inner.T)
    mapped = whitened[:kept]
    for iteration in range(ITERS):
        if iteration:
            mapped = contract_fast(mapped, whitened, 1, 0)
        gram = (contract if iteration + 1 == ITERS else contract_fast)(mapped, mapped, 1, 1)
        gram = jnp.concatenate([gram, jnp.zeros((kept, 128 - kept), jnp.float32)], axis=1)
        mapped = eliminate(jnp.concatenate([gram, mapped], axis=1), 0)[:, 128:]
    subspace = mapped[:, :size]
    forward = contract_fast(subspace, inverse, 1, 0)
    backward = contract_fast(subspace, upper, 1, 0)
    filter_matrix = contract_fast(forward, backward, 0, 0)
    filter_ref[...] = filter_matrix[:size, :size]
    narrow_ref[...] = filter_matrix.T[:size, :size].astype(jnp.bfloat16)


def mnf_filter(packed, size, signal_count, noise_count, kept):
    wide = packed.shape[0]
    return pl.pallas_call(
        functools.partial(mnf_kernel, 1.0 / signal_count, 1.0 / noise_count, kept),
        out_shape=[
            jax.ShapeDtypeStruct((size, size), jnp.float32),
            jax.ShapeDtypeStruct((size, size), jnp.bfloat16),
        ],
        in_specs=[pl.BlockSpec(memory_space=pltpu.VMEM)],
        out_specs=[pl.BlockSpec(memory_space=pltpu.VMEM)] * 2,
        scratch_shapes=[
            pltpu.VMEM((size, 2 * wide), jnp.float32), pltpu.VMEM((wide, wide), jnp.float32),
        ],
        name="mnf_filter",
    )(packed)


MESH = pl.DeviceIdType.MESH
VMEM_SPEC = pl.BlockSpec(memory_space=pltpu.VMEM)


def signal(semaphore, device):
    pl.semaphore_signal(semaphore, inc=1, device_id=device, device_id_type=MESH)


def merge(first, second, count):
    gap = second[0] - first[0]
    return first[0] + 0.5 * gap, first[1] + second[1] + (0.5 * count) * gap * gap


LIMIT = 40.0
FINE = 16.0
MEAN_STEP = 240.0 / math.log2(1.0 + LIMIT * FINE)
SPREAD_LOW, SPREAD_HIGH = math.log2(EPSILON), math.log2(LIMIT * LIMIT + 50.0)
SPREAD_STEP = 240.0 / (SPREAD_HIGH - SPREAD_LOW)
SPREAD_BASE = -0.5 * SPREAD_STEP * (SPREAD_HIGH + SPREAD_LOW)


def write_pair(ref, pair, count, *index):
    mean, total = pair
    code = jnp.exp2(MEAN_STEP * jnp.log2(1.0 + FINE * jnp.abs(mean)) - 120.0)
    ref[(*index, 0)] = jnp.where(mean < 0.0, -code, code).astype(ref.dtype)
    level = jnp.log2(total * (1.0 / count))
    ref[(*index, 1)] = jnp.exp2(SPREAD_STEP * level + SPREAD_BASE).astype(ref.dtype)


def read_codes(ref, *index):
    code = ref[(*index, 0)].astype(jnp.float32)
    size = jnp.exp2((jnp.log2(jnp.abs(code)) + 120.0) * (1.0 / MEAN_STEP)) - 1.0
    mean = jnp.where(code < 0.0, -size, size) * (1.0 / FINE)
    level = jnp.log2(ref[(*index, 1)].astype(jnp.float32)) - SPREAD_BASE
    return mean, level * (1.0 / SPREAD_STEP)


def read_pair(ref, count, *index):
    mean, level = read_codes(ref, *index)
    return mean, jnp.exp2(level) * count


def stats_part(
    lines, tracks, x_ref, mean_ref, spread_ref, ahead_ref,
    out0, in0, own, out1, in1, out2, in2, gathered, other, passing, send, recv, row_sem,
):
    chips = tracks // 2
    depth = chips // 2
    rows, bands, columns = x_ref.shape
    half = bands // 2
    width = in0.shape[-1]
    line = lax.axis_index("line")
    track = lax.axis_index("track")
    core, chip = lax.rem(track, 2), lax.div(track, 2)
    side, place = lax.rem(chip, 2), lax.div(chip, 2)
    own_rows = pl.ds(pl.multiple_of(core * half, 16), half)
    other_rows = pl.ds(pl.multiple_of((1 - core) * half, 16), half)
    partner = (line, chip * 2 + 1 - core)
    across = (line, (place * 2 + 1 - side) * 2 + core)

    def along(step):
        spot = lax.rem(place + step, depth)
        return spot, (line, (spot * 2 + side) * 2 + core)

    def copy(source, target, phase, sent, landed, device):
        return pltpu.make_async_remote_copy(
            src_ref=source, dst_ref=target, send_sem=send.at[phase, sent],
            recv_sem=recv.at[phase, landed], device_id=device, device_id_type=MESH,
        )

    def row_copy(source, target, sent, landed, device):
        return pltpu.make_async_remote_copy(
            src_ref=source, dst_ref=target, send_sem=row_sem.at[0, sent],
            recv_sem=row_sem.at[1, landed], device_id=device, device_id_type=MESH,
        )

    inner, outer = core == 1, core == 0
    low_side, high_side = side == 0, side == 1
    hands_down = outer & low_side & (place > 0)
    passes_on = inner & low_side & (place < depth - 1)
    has_after = track < tracks - 1
    below = (line, (place * 2 - 2) * 2 + 1)
    above = (line, (place * 2 + 2) * 2)
    beyond = (line, place * 4 + 1)
    to_partner = row_copy(x_ref.at[0], ahead_ref, 0, 0, partner)
    to_below = row_copy(x_ref.at[0], passing, 1, 1, below)
    to_across = row_copy(passing, ahead_ref, 1, 0, across)
    to_beyond = row_copy(x_ref.at[0], ahead_ref, 0, 0, beyond)

    barrier = pltpu.get_barrier_semaphore()
    signal(barrier, partner)
    signal(barrier, across)
    for step in range(1, depth):
        signal(barrier, along(step)[1])

    plane = lines * 2
    for step in range(1, plane):
        spot = lax.rem(line * 2 + side + step, plane)
        signal(barrier, (lax.div(spot, 2), (place * 2 + lax.rem(spot, 2)) * 2 + core))

    @pl.when(outer & high_side)
    def _():
        signal(barrier, beyond)

    @pl.when(inner & low_side)
    def _():
        signal(barrier, (line, place * 4 + 2))

    @pl.when(hands_down)
    def _():
        signal(barrier, below)

    @pl.when(passes_on)
    def _():
        signal(barrier, above)

    def local(band_rows, q):
        low = q * width
        high = min(low + width, columns)
        values = [x_ref[r, band_rows, low:high].astype(jnp.float32) for r in range(rows)]
        mean = sum(values[1:], values[0]) * (1.0 / rows)
        gaps = [value - mean for value in values]
        pair = mean, sum([gap * gap for gap in gaps], rows * EPSILON)
        if high - low < width:
            blank = jnp.ones((half, width - high + low), jnp.float32)
            pair = tuple(jnp.concatenate([item, blank], axis=1) for item in pair)
        return pair

    for q in range(chips):
        write_pair(out0, local(other_rows, q), rows, q)
    greeted = (outer & high_side) | (inner & low_side)
    relayed = hands_down | passes_on
    pl.semaphore_wait(
        barrier, depth + plane + greeted.astype(jnp.int32) + relayed.astype(jnp.int32)
    )

    @pl.when(hands_down)
    def _():
        to_below.start()


    started = []

    def launch(item):
        item.start()
        started.append(item)

    far = [(lax.rem(place + step, depth)) for step in range(1, depth + 1)]
    order = [spot * 2 + 1 - side for spot in far] + [spot * 2 + side for spot in far]
    for q in order:
        launch(copy(out0.at[q], in0.at[q], 0, q, q, partner))
    for q in range(chips):
        for k, item in enumerate(local(own_rows, q)):
            own[q, k] = item
    for spot in far:
        q = spot * 2 + 1 - side
        copy(in0.at[q], in0.at[q], 0, q, q, partner).wait_recv()
        pair = merge((own[q, 0], own[q, 1]), read_pair(in0, rows, q), rows)
        write_pair(out1, pair, 2 * rows, spot)
        launch(copy(out1.at[spot], in1.at[spot], 1, spot, spot, across))

    @pl.when(inner)
    def _():
        to_partner.start()

    @pl.when(outer & high_side)
    def _():
        to_beyond.start()

    @pl.when(passes_on)
    def _():
        row_copy(x_ref.at[0], passing, 1, 1, above).wait_recv()
        to_across.start()

    for step, spot in enumerate(far, 1):
        q = spot * 2 + side
        copy(in0.at[q], in0.at[q], 0, q, q, partner).wait_recv()
        pair = merge((own[q, 0], own[q, 1]), read_pair(in0, rows, q), rows)
        copy(in1.at[spot], in1.at[spot], 1, spot, spot, across).wait_recv()
        pair = merge(pair, read_pair(in1, 2 * rows, spot), 2 * rows)
        if step < depth:
            write_pair(out2, pair, 4 * rows, spot)
            launch(copy(out2.at[spot], in2.at[place], 2, spot, place, along(step)[1]))
    groups = [pair]
    for step in range(1, depth):
        spot, peer = along(step)
        copy(in2.at[spot], in2.at[spot], 2, spot, spot, peer).wait_recv()
        groups.append(read_pair(in2, 4 * rows, spot))
    mean = sum([group[0] for group in groups[1:]], groups[0][0]) * (1.0 / depth)
    total = sum([group[1] for group in groups[1:]], groups[0][1])
    for group in groups:
        total = total + (4.0 * rows) * (group[0] - mean) * (group[0] - mean)
    write_pair(gathered, (mean, total), tracks * rows, chip)

    def relay(q):
        launch(copy(gathered.at[q], other.at[q], 5, q, q, partner))

    def settle(ref, q, band_rows):
        mean, level = read_codes(ref, q)
        mean_ref[q, band_rows, :] = mean
        spread_ref[q, band_rows, :] = jnp.exp2(0.5 * level)

    for step in range(1, depth):
        launch(copy(gathered.at[chip], gathered.at[chip], 3, step, chip, along(step)[1]))
    for step in range(depth):
        spot, peer = along(step)
        q = spot * 2 + side
        if step:
            copy(gathered.at[q], gathered.at[q], 3, q, q, peer).wait_recv()
        launch(copy(gathered.at[q], gathered.at[q], 4, q, q, across))
        relay(q)
        settle(gathered, q, own_rows)
    for step in range(depth):
        q = along(step)[0] * 2 + 1 - side
        copy(gathered.at[q], gathered.at[q], 4, q, q, across).wait_recv()
        relay(q)
        settle(gathered, q, own_rows)
    for last in (side, 1 - side):
        for step in range(depth):
            q = along(step)[0] * 2 + last
            copy(other.at[q], other.at[q], 5, q, q, partner).wait_recv()
            settle(other, q, other_rows)

    @pl.when(has_after)
    def _():
        to_partner.wait_recv()

    @pl.when(jnp.logical_not(has_after))
    def _():
        ahead_ref[...] = x_ref[0]

    def finish():
        for item in started:
            item.wait_send()

        @pl.when(inner)
        def _():
            to_partner.wait_send()

        @pl.when(outer & high_side)
        def _():
            to_beyond.wait_send()

        @pl.when(hands_down)
        def _():
            to_below.wait_send()

        @pl.when(passes_on)
        def _():
            to_across.wait_send()

    return finish


def centre_part(
    keep, x_ref, mean_ref, spread_ref, ahead_ref, work, band_ref, packed_ref, change,
):
    rows, bands, columns = x_ref.shape
    chips, _, width = mean_ref.shape
    band_mean = jnp.zeros((bands, 1), jnp.float32)
    band_spread = jnp.zeros((bands, 1), jnp.float32)
    for q in range(chips):
        span = min(width, columns - q * width)
        band_mean += jnp.sum(mean_ref[q, :, :span], axis=1, keepdims=True)
        band_spread += jnp.sum(spread_ref[q, :, :span], axis=1, keepdims=True)
    band_ref[...] = band_mean * (1.0 / columns)
    band_spread = band_spread * (1.0 / columns)
    for q in range(chips):
        low = q * width
        high = min(low + width, columns)
        span = high - low
        mean = mean_ref[q, :, :span]
        factor = band_spread / spread_ref[q, :, :span]

        def rounded(values):
            return ((values.astype(jnp.float32) - mean) * factor).astype(jnp.bfloat16)

        now = rounded(x_ref[0, :, low:high])
        for r in range(rows):
            work[r, :, low:high] = now
            later = rounded(x_ref[r + 1, :, low:high] if r + 1 < rows else ahead_ref[:, low:high])
            step = later.astype(jnp.float32) - now.astype(jnp.float32)
            if r + 1 == rows:
                step = step * keep
            change[r, :, low:high] = step.astype(jnp.bfloat16)
            now = later
    full = chips * width
    if full > columns:
        blank = jnp.zeros((rows, bands, full - columns), jnp.bfloat16)
        work[:, :, columns:] = blank
        change[:, :, columns:] = blank

    def gram(ref):
        total = jnp.zeros((bands, bands), jnp.float32)
        for r in range(rows):
            total += lax.dot_general(
                ref[r], ref[r], (((1,), (1,)), ((), ())), preferred_element_type=jnp.float32
            )
        return total

    signal_part, noise_part = gram(work), gram(change)
    row_ids = lax.broadcasted_iota(jnp.int32, (bands, bands), 0)
    column_ids = lax.broadcasted_iota(jnp.int32, (bands, bands), 1)
    diagonal = jnp.sum(
        jnp.where(row_ids == column_ids, signal_part, 0.0), axis=0, keepdims=True
    )
    square = jnp.where(row_ids < column_ids, signal_part, noise_part)
    halves, plane, depth, _ = packed_ref.shape
    packed_ref[...] = jnp.zeros(packed_ref.shape, jnp.float32)
    for piece in range(halves * plane):
        half, spot = divmod(piece, plane)
        low = piece * depth
        live = min(depth, bands - low)
        if live > 0:
            packed_ref[half, spot, :live, :bands] = square[low:low + live]
        if low <= bands < low + depth:
            packed_ref[half, spot, bands - low:bands - low + 1, :bands] = diagonal


def gram_part(lines, tracks, x_ref, out_ref, in0, mine, in1, total, in2, gathered, in3, send, recv):
    depth = tracks // 4
    line = lax.axis_index("line")
    track = lax.axis_index("track")
    core, chip = lax.rem(track, 2), lax.div(track, 2)
    side, place = lax.rem(chip, 2), lax.div(chip, 2)
    plane = lines * 2
    me = line * 2 + side
    partner = (line, chip * 2 + 1 - core)

    def beside(step):
        spot = lax.rem(me + step, plane)
        return spot, (lax.div(spot, 2), (place * 2 + lax.rem(spot, 2)) * 2 + core)

    def along(step):
        spot = lax.rem(place + step, depth)
        return spot, (line, (spot * 2 + side) * 2 + core)

    def copy(source, target, phase, sent, landed, device):
        return pltpu.make_async_remote_copy(
            src_ref=source, dst_ref=target, send_sem=send.at[phase, sent],
            recv_sem=recv.at[phase, landed], device_id=device, device_id_type=MESH,
        )

    started = []

    def launch(item):
        item.start()
        started.append(item)

    for step in range(1, plane + 1):
        spot = beside(step)[0]
        launch(copy(x_ref.at[1 - core, spot], in0.at[spot], 0, spot, spot, partner))
    for step in range(1, plane + 1):
        spot, peer = beside(step)
        copy(in0.at[spot], in0.at[spot], 0, spot, spot, partner).wait_recv()
        mine[spot] = x_ref[core, spot] + in0[spot]
        if step < plane:
            launch(copy(mine.at[spot], in1.at[me], 1, spot, me, peer))
    piece = mine[me]
    for step in range(1, plane):
        spot, peer = beside(step)
        copy(in1.at[spot], in1.at[spot], 1, spot, spot, peer).wait_recv()
        piece = piece + in1[spot]
    total[...] = piece
    in2[place] = piece
    for step in range(1, depth):
        spot, peer = along(step)
        launch(copy(total, in2.at[place], 2, spot, place, peer))
    for step in range(1, depth):
        spot, peer = along(step)
        copy(in2.at[spot], in2.at[spot], 2, spot, spot, peer).wait_recv()
    piece = in2[0]
    for spot in range(1, depth):
        piece = piece + in2[spot]
    gathered[me] = piece
    for step in range(1, plane):
        launch(copy(gathered.at[me], gathered.at[me], 3, step, me, beside(step)[1]))
    launch(copy(gathered.at[me], in3.at[me], 4, me, me, partner))
    out_ref[core, me] = piece
    for step in range(1, plane):
        spot, peer = beside(step)
        copy(gathered.at[spot], gathered.at[spot], 3, spot, spot, peer).wait_recv()
        launch(copy(gathered.at[spot], in3.at[spot], 4, spot, spot, partner))
        out_ref[core, spot] = gathered[spot]
    for step in range(plane):
        spot = beside(step)[0]
        copy(in3.at[spot], in3.at[spot], 4, spot, spot, partner).wait_recv()
        out_ref[1 - core, spot] = in3[spot]
    for item in started:
        item.wait_send()


def campaign_kernel(lines, tracks, x_ref, centred_ref, band_ref, total_ref, *scratch):
    mean, spread, ahead, change, packed = scratch[:5]
    gram_scratch, stats_scratch = scratch[5:14], scratch[14:]
    finish = stats_part(lines, tracks, x_ref, mean, spread, ahead, *stats_scratch)
    keep = jnp.where(lax.axis_index("track") < tracks - 1, 1.0, 0.0)
    centre_part(keep, x_ref, mean, spread, ahead, centred_ref, band_ref, packed, change)
    gram_part(lines, tracks, packed, total_ref, *gram_scratch)
    finish()


def campaign(local_block, lines, tracks, height, wide):
    chips, plane = tracks // 2, lines * 2
    depth = chips // 2
    rows, bands, columns = local_block.shape
    width = -(-columns // (128 * chips)) * 128
    full = chips * width
    half = bands // 2
    piece = (height // (2 * plane), wide)

    def buffer(count, dtype=jnp.bfloat16):
        return pltpu.VMEM((count, 2, half, width), dtype)

    stack = pltpu.VMEM((plane,) + piece, jnp.float32)
    centred, band_mean, total = pl.pallas_call(
        functools.partial(campaign_kernel, lines, tracks),
        out_shape=[
            jax.ShapeDtypeStruct((rows, bands, full), jnp.bfloat16),
            jax.ShapeDtypeStruct((bands, 1), jnp.float32),
            jax.ShapeDtypeStruct((2, plane) + piece, jnp.float32),
        ],
        in_specs=[VMEM_SPEC],
        out_specs=[VMEM_SPEC] * 3,
        scratch_shapes=[pltpu.VMEM((chips, bands, width), jnp.float32)] * 2
        + [pltpu.VMEM((bands, columns), jnp.bfloat16)]
        + [pltpu.VMEM((rows, bands, full), jnp.bfloat16)]
        + [pltpu.VMEM((2, plane) + piece, jnp.float32)]
        + [stack, stack, stack, pltpu.VMEM(piece, jnp.float32)]
        + [pltpu.VMEM((depth,) + piece, jnp.float32), stack, stack]
        + [pltpu.SemaphoreType.DMA((5, max(plane, depth)))] * 2
        + [buffer(chips), buffer(chips), buffer(chips, jnp.float32)]
        + [buffer(depth)] * 4 + [buffer(chips)] * 2
        + [pltpu.VMEM((bands, columns), jnp.bfloat16)]
        + [pltpu.SemaphoreType.DMA((6, chips))] * 2 + [pltpu.SemaphoreType.DMA((2, 2))],
        compiler_params=pltpu.CompilerParams(collective_id=0, has_side_effects=True),
        name="campaign",
    )(local_block)
    return centred, band_mean, total.reshape(height, wide)


def restore_kernel(narrow_ref, band_ref, centred_ref, cleaned_ref):
    mixed = jnp.dot(narrow_ref[...], centred_ref[0], preferred_element_type=jnp.float32)
    cleaned_ref[0] = (band_ref[...] + mixed[:, :cleaned_ref.shape[2]]).astype(jnp.bfloat16)


def restore(narrow, band_mean, centred, columns):
    rows, bands, full = centred.shape
    return pl.pallas_call(
        restore_kernel,
        grid=(rows,),
        out_shape=jax.ShapeDtypeStruct((rows, bands, columns), jnp.bfloat16),
        in_specs=[
            pl.BlockSpec((bands, bands), lambda r: (0, 0)),
            pl.BlockSpec((bands, 1), lambda r: (0, 0)),
            pl.BlockSpec((1, bands, full), lambda r: (r, 0, 0)),
        ],
        out_specs=pl.BlockSpec((1, bands, columns), lambda r: (r, 0, 0)),
        name="restore",
    )(narrow, band_mean, centred)


def body(radiance):
    local_block = radiance[0]
    row_count, size, column_count = local_block.shape
    track_count = lax.axis_size("track")
    line_count = lax.axis_size("line")
    total_rows = row_count * track_count
    wide = (size // 128 + 1) * 128
    pieces = 16 * 2 * line_count
    height = -(-max(size + 1, wide) // pieces) * pieces
    centred, band_mean, packed = campaign(local_block, line_count, track_count, height, wide)
    packed = packed[:wide]
    signal_count = line_count * total_rows * column_count
    noise_count = 2 * line_count * (total_rows - 1) * column_count
    filter_matrix, narrow = mnf_filter(packed, size, signal_count, noise_count, NCOMP)
    cleaned = restore(narrow, band_mean, centred, column_count)
    return (cleaned[None], filter_matrix)


def solution(mesh):
    in_specs = (P("line", "track", None, None),)
    out_specs = (P("line", "track", None, None), P())
    return jax.shard_map(body, mesh=mesh, in_specs=in_specs, out_specs=out_specs, check_vma=False)
```
